32 devices in a mesh: ctx: 16 (over z, y, x), ch: 2 (over core).
Axes of the slice: x: 2, y: 2, z: 4, core: 2. Of those that a mesh axis runs over, the one named last changes fastest.
Arguments:
- tokens: bfloat16 [16384, 8192], P('ctx', 'ch'), may hold values from -6 to 6
- in_weight: bfloat16 [128, 3, 8192], P('ctx', None, 'ch'), may hold values from -0.09375 to 0.09375
- conv_filter: float32 [128, 16384], P('ch', 'ctx'), as said below
- skip_gain: float32 [128], P('ch'), may hold values from -4 to 4
- group_order: int32 [32], replicated, may hold values from 0 to 31, each once
- out_weight: bfloat16 [128, 8192], P('ctx', 'ch'), may hold values from -0.5 to 0.5
Outputs:
- mixed: bfloat16 [16384, 8192], P('ctx', 'ch')
The draws below stay inside these ranges and needn't reach their ends.
Inputs may be any that keep to these rules, and one draw needn't show every extreme that they name: `conv_filter`: each channel's filter has a sum of squares of one over all 16384 lags. `group_order`: a permutation of the storage blocks' group numbers.
All inputs are finite; a program needn't handle non-finite values.
Results may differ from the reference program's by a relative error of at most 0.0049.
Values may be sent and summed in bfloat16 or wider, within the bound.
A program may use at most 192 MiB of HBM per device.

```python
import math
import jax
import jax.numpy as jnp
from jax import lax

D = 8192
C = 128
SEQ = 16384
GROUP = 512
BLOCKS = 32


def draw_conv_filter(key, part):
    keys = jax.random.split(jax.random.fold_in(key, 7), 5)
    lags = jnp.arange(SEQ, dtype=jnp.float32)
    share = 0.5
    picks = jax.random.uniform(keys[0], (C,), jnp.float32)
    fast = jnp.exp(jax.random.uniform(keys[1], (C,), jnp.float32, math.log(30.0), math.log(50.0)))
    slow = jnp.exp(jax.random.uniform(keys[2], (C,), jnp.float32, math.log(SEQ / 2.0), math.log(8.0 * SEQ)))
    spans = jnp.where(picks < share, slow, fast)
    envelope = jnp.exp(-lags[None, :] / spans[:, None])
    noise = jax.random.truncated_normal(keys[3], -4.0, 4.0, (C, SEQ), jnp.float32)
    noise = noise * jax.random.uniform(keys[4], (C, SEQ), jnp.float32, 0.5, 1.5)
    shaped = noise * envelope
    energy = jnp.sum(shaped * shaped, axis=1)
    return (shaped / jnp.sqrt(energy)[:, None]).astype(jnp.float32)


def raised(entries, own_key, source, target, shards_of, factor):
    def block_of(dim):
        return (jnp.arange(entries.shape[dim]) // (entries.shape[dim] // shards_of)).reshape((-1,) + (1,) * (entries.ndim - 1 - dim))

    first = jax.random.permutation(own_key, shards_of)[block_of(target)]
    far = (block_of(target) + shards_of // 2) % shards_of
    return jnp.where((block_of(source) == first) | (block_of(source) == far), factor * entries, entries)


def steps_of(stream_key, extent, pieces, low, high):
    def one(dim, parts):
        steps = jax.random.uniform(jax.random.fold_in(jax.random.fold_in(stream_key, 6), dim), (parts,), jnp.float32, low / len(pieces), high / len(pieces))
        return jnp.repeat(jnp.exp(steps), extent[dim] // parts).reshape((-1,) + (1,) * (len(extent) - dim - 1))

    loudness = one(*pieces[0])
    for cut in pieces[1:]:
        loudness = loudness * one(*cut)
    return loudness


def centred(key, extent, scale, most, shards=(), kind=jnp.bfloat16):
    drawn = jax.random.normal(key, extent, jnp.float32) * scale
    if len(shards) > 0:
        drawn = steps_of(key, extent, shards, -0.22, 0.18) * drawn
    return jnp.clip(drawn, min=-most, max=most).astype(kind)


def heavy_noise(own_key, extent, scale, limit, pieces, heavy, kind=jnp.bfloat16):
    values = scale * jax.random.normal(own_key, extent, jnp.float32)
    if pieces:
        values = values * steps_of(own_key, extent, pieces, -0.22, 0.18)
    return jnp.clip(raised(values, jax.random.fold_in(own_key, 3), *heavy), -limit, limit).astype(kind)


def setup_inputs(seed: int = 0) -> dict:
    arg_keys = jax.random.split(jax.random.key(seed), 7)
    return {
        "tokens": centred(arg_keys[0], (SEQ, D), 1.0, 6.0, ((0, 16), (1, 2))),
        "in_weight": heavy_noise(arg_keys[1], (C, 3, D), D ** -0.5, 0.09375, ((0, 16), (2, 2)), (2, 0, 16, 2.0)),
        "conv_filter": draw_conv_filter(jax.random.fold_in(arg_keys[6], 71), 0),
        "skip_gain": centred(arg_keys[3], (C,), 1.0, 4.0, ((0, 2),), jnp.float32),
        "group_order": jax.random.permutation(arg_keys[4], BLOCKS).astype(jnp.int32),
        "out_weight": centred(arg_keys[5], (C, D), C ** -0.5, 0.5, ((0, 16), (1, 2))),
    }


def reference(tokens, in_weight, conv_filter, skip_gain, group_order, out_weight):
    flat = in_weight.reshape(3 * C, D)
    token_blocks = tokens.reshape(BLOCKS, GROUP, D)

    def project(block):
        return lax.dot_general(flat, block, (((1,), (1,)), ((), ())), preferred_element_type=jnp.float32)

    proj = lax.map(project, token_blocks)
    proj = jnp.transpose(proj, (1, 0, 2)).reshape(C, 3, SEQ)
    gate_part = proj[:, 0]
    product = proj[:, 1] * proj[:, 2]
    inverse = jnp.zeros((BLOCKS,), jnp.int32).at[group_order].set(jnp.arange(BLOCKS, dtype=jnp.int32))
    in_sequence = product.reshape(C, BLOCKS, GROUP)[:, inverse].reshape(C, SEQ)
    length = 2 * SEQ
    spectrum = jnp.fft.rfft(in_sequence, length, axis=1) * jnp.fft.rfft(conv_filter, length, axis=1)
    conv_seq = jnp.fft.irfft(spectrum, length, axis=1)[:, :SEQ]
    conv = conv_seq.reshape(C, BLOCKS, GROUP)[:, group_order].reshape(C, SEQ)
    hidden = (gate_part * (conv + skip_gain[:, None] * product)).astype(jnp.bfloat16)
    hidden_blocks = jnp.transpose(hidden.reshape(C, BLOCKS, GROUP), (1, 0, 2))

    def output(block):
        result = lax.dot_general(block, out_weight, (((0,), (0,)), ((), ())), preferred_element_type=jnp.float32)
        return result.astype(jnp.bfloat16)

    return lax.map(output, hidden_blocks).reshape(SEQ, D)
```

```python
import math

import jax
import jax.numpy as jnp
from jax import lax
from jax.sharding import PartitionSpec as P

high = lax.Precision.HIGH


def split_length(length):
    cols = 1 << ((length.bit_length() - 1) // 2)
    return length // cols, cols


def cos_sin(numer, period):
    angle = (numer % period).astype(jnp.float32) * (2.0 * math.pi / period)
    return jnp.cos(angle), jnp.sin(angle)


def row_table(row_ids, rows):
    freq = 4 * jnp.arange(rows, dtype=jnp.int32) + 1
    cos, sin = cos_sin(freq[:, None] * row_ids[None, :], 4 * rows)
    return jnp.concatenate([cos, -sin], axis=0)


def col_table(cols):
    ids = jnp.arange(cols, dtype=jnp.int32)
    cos, sin = cos_sin(ids[:, None] * ids[None, :], cols)
    top = jnp.concatenate([cos, -sin], axis=1)
    bottom = jnp.concatenate([sin, cos], axis=1)
    return jnp.concatenate([top, bottom], axis=0)


def twist(rows, cols):
    freq = 4 * jnp.arange(rows, dtype=jnp.int32) + 1
    return cos_sin(freq[:, None] * jnp.arange(cols, dtype=jnp.int32)[None, :], 4 * rows * cols)


def spectrum(values, row_dft, col_dft, tw):
    rows, chans, cols = values.shape
    cos, sin = tw[0][:, None, :], tw[1][:, None, :]
    part = jnp.dot(row_dft, values.reshape(rows, chans * cols), precision=high)
    real = part[:rows].reshape(rows, chans, cols)
    imag = part[rows:].reshape(rows, chans, cols)
    turned = jnp.concatenate([real * cos + imag * sin, imag * cos - real * sin], axis=2)
    out = jnp.dot(turned.reshape(rows * chans, 2 * cols), col_dft, precision=high)
    return out.reshape(rows, chans, 2 * cols)


def causal_conv(values, taps, row_ids):
    rows, chans, cols = values.shape
    col_dft = col_table(cols)
    tw = twist(rows, cols)
    perm_dft = row_table(row_ids, rows)
    sig = spectrum(values, perm_dft, col_dft, tw)
    fil = spectrum(taps, row_table(jnp.arange(rows, dtype=jnp.int32), rows), col_dft, tw)
    sr, si = sig[..., :cols], sig[..., cols:]
    fr, fi = fil[..., :cols], fil[..., cols:]
    both = jnp.concatenate([sr * fr - si * fi, sr * fi + si * fr], axis=2)
    back = jnp.dot(both.reshape(rows * chans, 2 * cols), col_dft.T, precision=high)
    back = back.reshape(rows, chans, 2 * cols) * (1.0 / (rows * cols))
    br, bi = back[..., :cols], back[..., cols:]
    cos, sin = tw[0][:, None, :], tw[1][:, None, :]
    turned = jnp.concatenate([br * cos - bi * sin, br * sin + bi * cos], axis=0)
    out = jnp.dot(perm_dft.T, turned.reshape(2 * rows, chans * cols), precision=high)
    return out.reshape(rows, chans, cols)


def per_device(tokens, in_weight, conv_filter, skip_gain, group_order, out_weight):
    ctx = lax.axis_size("ctx")
    ch = lax.axis_size("ch")
    tok_count, feat_local = tokens.shape
    chan_local = conv_filter.shape[0]
    seq = tok_count * ctx
    group = seq // group_order.shape[0]
    rows, cols = split_length(seq)
    own_rows = tok_count // cols
    owned = -(-chan_local // ctx)
    padded = owned * ctx

    def outward(signal):
        signal = jnp.pad(signal, ((0, padded - chan_local), (0, 0)))
        parts = signal.reshape(ctx, owned, own_rows, cols).transpose(0, 2, 1, 3)
        got = lax.all_to_all(parts, "ctx", split_axis=0, concat_axis=0, tiled=True)
        return got.reshape(rows, owned, cols)

    taps = outward(conv_filter)
    mine = in_weight.reshape(-1, feat_local)
    flat = lax.all_gather(mine, "ctx", axis=0, tiled=True)
    partial = lax.dot_general(flat, tokens, (((1,), (1,)), ((), ())), preferred_element_type=jnp.float32)
    if ch == 2:
        me = lax.axis_index("ch")
        half = partial.shape[0] // 2
        away = lax.dynamic_slice_in_dim(partial, (1 - me) * half, half, 0)
        kept = lax.dynamic_slice_in_dim(partial, me * half, half, 0)
        proj = kept + lax.ppermute(away, "ch", [(0, 1), (1, 0)])
    else:
        proj = lax.psum_scatter(partial, "ch", scatter_dimension=0, tiled=True)
    proj = proj.reshape(chan_local, 3, tok_count)
    gate = proj[:, 0]
    product = proj[:, 1] * proj[:, 2]
    in_group = jnp.arange(group // cols, dtype=jnp.int32)
    row_ids = (group_order[:, None] * (group // cols) + in_group[None, :]).reshape(rows)
    conv = causal_conv(outward(product), taps, row_ids)
    back = lax.all_to_all(
        conv.reshape(ctx, own_rows, owned, cols), "ctx", split_axis=0, concat_axis=0, tiled=True
    )
    conv = back.transpose(0, 2, 1, 3).reshape(padded, tok_count)[:chan_local]
    hidden = (gate * (conv + skip_gain[:, None] * product)).astype(jnp.bfloat16)
    hidden_all = lax.all_gather(hidden, "ch", axis=0, tiled=True)
    rows_all = lax.all_gather(out_weight, "ctx", axis=0, tiled=True)
    mixed = lax.dot_general(
        hidden_all, rows_all, (((0,), (0,)), ((), ())), preferred_element_type=jnp.float32
    )
    return mixed.astype(jnp.bfloat16)


def solution(mesh):
    in_specs = (P("ctx", "ch"), P("ctx", None, "ch"), P("ch", "ctx"), P("ch"), P(), P("ctx", "ch"))
    return jax.shard_map(
        per_device, mesh=mesh, in_specs=in_specs, out_specs=P("ctx", "ch"), check_vma=False
    )
```
